32 devices in a mesh: stick: 2 (over x), band: 16 (over z, y, core).
Axes of the slice: x: 2, y: 2, z: 4, core: 2. Of those that a mesh axis runs over, the one named last changes fastest.
Arguments:
- orbital_sticks: bfloat16 [32, 6144, 128], P('band', 'stick'), may hold values from -5 to 5
- stick_perm: int32 [4096], replicated, may hold values from 0 to 4095, each once
- stick_counts: int32 [2], replicated, may hold values from 1 to 3072, 4096 in all
- source_ids: int32 [1], replicated, may hold values from 0 to 31
Outputs:
- exchange: bfloat16 [32, 64, 64, 128], P(('band', 'stick'))
The draws below stay inside these ranges and needn't reach their ends.
All inputs are finite; a program needn't handle non-finite values.
Results may differ from the reference program's by a relative error of at most 0.001.
Values may be sent and summed in bfloat16 or wider, within the bound.
A program may use at most 64 MiB of HBM per device.

```python
import math
import jax
import jax.numpy as jnp
import numpy as np
from jax import lax

NX = 64
NY = 64
NZ = 128
NSRC = 1
NB = 32
NXY = 4096
CAP = 3072
SLOTS = 6144
N_STICK = 2


def block_scale(rng, extent, split, smallest, largest):
    factor_of, own = 1.0, jax.random.fold_in(rng, 6)
    for dim, blocks in split:
        steps = jnp.exp(jax.random.uniform(jax.random.fold_in(own, dim), (blocks,), jnp.float32, smallest / len(split), largest / len(split)))
        factor_of = factor_of * jnp.repeat(steps, extent[dim] // blocks).reshape([-1 if axis == dim else 1 for axis in range(len(extent))])
    return factor_of


def profile(amount, total, reach, slope):
    portions = [(1 << 20) // math.isqrt(rank ** slope) + 1 for rank in range(2, amount + 1)]
    spare, given = total - reach - (amount - 1), [1] * (amount - 1)
    while spare > 0:
        movable = [i for i in range(amount - 1) if given[i] < reach]
        pool, remaining = sum([portions[i] for i in movable]), spare
        for i in movable:
            extra = min(reach - given[i], max(1, remaining * portions[i] // pool), spare)
            given[i] = given[i] + extra
            spare = spare - extra
    return np.array([reach] + given)


def ragged(stream_key, number_of, total, bound, skew):
    if number_of == 2:
        one = jax.random.randint(stream_key, (), max(1, total - bound), min(bound, total - 1) + 1)
        return jnp.stack([one, total - one])
    tallies = jnp.asarray(profile(number_of, total, bound, skew), jnp.int32)
    twos = (number_of - 1) // 2
    source_of, sink = tallies[1:1 + 2 * twos:2], tallies[2:2 + 2 * twos:2]
    slack = jnp.minimum(source_of - 1, bound - sink)
    passed = jax.random.randint(jax.random.fold_in(stream_key, 1), (twos,), 0, 1 << 20) % (slack + 1)
    tallies = tallies.at[1:1 + 2 * twos:2].set(source_of - passed).at[2:2 + 2 * twos:2].set(sink + passed)
    return tallies[jax.random.permutation(jax.random.fold_in(stream_key, 2), number_of)]


def centred(key, shape, spread, reach, pieces=(), held_as=jnp.bfloat16):
    drawn = jax.random.normal(key, shape, jnp.float32) * spread
    if len(pieces) > 0:
        drawn = block_scale(key, shape, pieces, -0.22, 0.18) * drawn
    return jnp.clip(drawn, min=-reach, max=reach).astype(held_as)


def setup_inputs(seed: int = 0) -> dict:
    seeds = jax.random.split(jax.random.key(seed), 5)
    orbital_sticks = centred(seeds[0], (NB, SLOTS, NZ), 0.7, 5.0, ((0, 16), (1, 2)))
    stick_perm = jax.random.permutation(seeds[1], NXY).astype(jnp.int32)
    stick_counts = ragged(seeds[2], N_STICK, NXY, CAP, 2).astype(jnp.int32)
    source_ids = jax.random.randint(seeds[3], (NSRC,), 0, NB).astype(jnp.int32)
    return dict(orbital_sticks=orbital_sticks, stick_perm=stick_perm, stick_counts=stick_counts, source_ids=source_ids)


screen_omega = 0.25


def slot_targets(stick_perm, stick_counts):
    slots = jnp.arange(SLOTS, dtype=jnp.int32)
    holder = slots // CAP
    within = slots % CAP
    offsets = jnp.cumsum(stick_counts).astype(jnp.int32) - stick_counts
    valid = within < stick_counts[holder]
    position = jnp.clip(offsets[holder] + within, 0, NX * NY - 1).astype(jnp.int32)
    return jnp.where(valid, stick_perm[position], NX * NY).astype(jnp.int32)


def place_sticks(blocks, targets):
    empty = jnp.zeros((blocks.shape[0], NX * NY + 1, NZ), blocks.dtype)
    filled = empty.at[:, targets].set(blocks)
    return filled[:, :NX * NY].reshape(blocks.shape[0], NX, NY, NZ)


def signed_freq(length):
    steps = jnp.arange(length, dtype=jnp.int32)
    signed = jnp.where(steps <= length // 2, steps, steps - length)
    return signed.astype(jnp.float32) / length


def screened(freq_x, freq_y, freq_z):
    square = (2.0 * math.pi) ** 2 * (freq_x[:, None, None] ** 2 + freq_y[None, :, None] ** 2 + freq_z[None, None, :] ** 2)
    safe = jnp.where(square > 0, square, 1.0)
    inner = 4.0 * math.pi * (1.0 - jnp.exp(-square / (4.0 * screen_omega ** 2))) / safe
    return jnp.where(square > 0, inner, math.pi / screen_omega ** 2)


def reference(orbital_sticks, stick_perm, stick_counts, source_ids):
    targets = slot_targets(stick_perm, stick_counts)
    half_z = jnp.arange(NZ // 2 + 1, dtype=jnp.int32).astype(jnp.float32) / NZ
    kernel = screened(signed_freq(NX), signed_freq(NY), half_z)
    sources = place_sticks(orbital_sticks[source_ids], targets).astype(jnp.float32)

    def one_band(band):
        block = lax.dynamic_slice_in_dim(orbital_sticks, band, 1, 0)
        orbital = place_sticks(block, targets)[0].astype(jnp.float32)
        total = jnp.zeros((NX, NY, NZ), jnp.float32)
        for which in range(NSRC):
            density = orbital * sources[which]
            potential = jnp.fft.irfftn(jnp.fft.rfftn(density) * kernel, s=(NX, NY, NZ))
            total = total + sources[which] * potential
        return (-total).astype(jnp.bfloat16)

    return lax.map(one_band, jnp.arange(NB, dtype=jnp.int32))
```

```python
import functools
import math

import jax
import jax.numpy as jnp
import numpy as np
from jax import lax
from jax.experimental import pallas as pl
from jax.experimental.pallas import tpu as pltpu
from jax.sharding import PartitionSpec as P

NX = 64
NY = 64
NZ = 128
CHUNKS = 8

screen_omega = 0.25


def signed_freq(length):
    steps = np.arange(length, dtype=np.int32)
    signed = np.where(steps <= length // 2, steps, steps - length)
    return signed.astype(np.float64) / length


def screened(freq_x, freq_y, freq_z):
    square = (2.0 * math.pi) ** 2 * (
        freq_x[:, None, None] ** 2 + freq_y[None, :, None] ** 2 + freq_z[None, None, :] ** 2
    )
    safe = np.where(square > 0, square, 1.0)
    inner = 4.0 * math.pi * (1.0 - np.exp(-square / (4.0 * screen_omega**2))) / safe
    return np.where(square > 0, inner, math.pi / screen_omega**2)


def hartley_table(length):
    steps = np.arange(length, dtype=np.int64)
    angle = (steps[:, None] * steps[None, :] % length) * (2.0 * math.pi / length)
    return np.cos(angle) + np.sin(angle)


def halves(table):
    high = table.astype(jnp.bfloat16)
    low = (table - high.astype(np.float64)).astype(jnp.bfloat16)
    return high, low


def band_shape(bands):
    return (bands // 4, 2, 2) if bands % 4 == 0 else (bands, 1, 1)


def spread_kernel(root, sticks, shape, chunk, piece, mine, source, owned, local_sem, tree_send, tree_recv,
                  peer_send, peer_recv, core_send, core_recv, swap_send, swap_recv):
    lines, wide, cores = shape
    stick = lax.axis_index("stick")
    band = lax.axis_index("band")
    core = band % cores
    row = (band // cores) % wide
    line = band // (cores * wide)
    root_core = root % cores
    root_row = (root // cores) % wide
    root_line = root // (cores * wide)
    place = lambda l, r, c: (l * wide + r) * cores + c

    barrier = pltpu.get_barrier_semaphore()

    def greet(**where):
        pl.semaphore_signal(barrier, inc=1, device_id=where, device_id_type=pl.DeviceIdType.MESH)

    pl.when(line > 0)(lambda: greet(band=place(line - 1, row, core)))
    pl.when(line < lines - 1)(lambda: greet(band=place(line + 1, row, core)))
    for step in range(1, wide):
        greet(band=place(line, (row + step) % wide, core))
    for step in range(1, cores):
        greet(band=place(line, row, (core + step) % cores))
    for step in range(1, sticks):
        greet(stick=(stick + step) % sticks)
    near = jnp.where(line > 0, 1, 0) + jnp.where(line < lines - 1, 1, 0)
    pl.semaphore_wait(barrier, near + (wide - 1) + (cores - 1) + (sticks - 1))

    def remote(src, dst, send, recv, **where):
        return pltpu.make_async_remote_copy(
            src_ref=src, dst_ref=dst, send_sem=send, recv_sem=recv,
            device_id=where, device_id_type=pl.DeviceIdType.MESH)

    def swap(step, k):
        rows = pl.ds(pl.multiple_of(k * chunk, chunk), chunk)
        peer = (stick + step) % sticks
        return remote(mine.at[peer, rows], owned.at[stick, rows], swap_send.at[step, k], swap_recv.at[step, k],
                      stick=peer)

    keep = pltpu.make_async_copy(mine.at[stick], owned.at[stick], local_sem.at[0])
    keep.start()
    primary = core == root_core
    is_root = band == root
    held = pltpu.make_async_copy(piece, source.at[stick], local_sem.at[1])
    pl.when(is_root)(held.start)

    def tree(slot, k, target):
        rows = pl.ds(pl.multiple_of(k * chunk, chunk), chunk)
        return lambda src: remote(src.at[rows], source.at[stick, rows], tree_send.at[slot, k], tree_recv.at[k],
                                  band=target)

    up_ok = primary & (row == root_row) & (line >= root_line) & (line < lines - 1)
    down_ok = primary & (row == root_row) & (line <= root_line) & (line > 0)
    side_ok = primary & (row == root_row)
    exits = [(up_ok, place(line + 1, row, core)), (down_ok, place(line - 1, row, core))]
    exits += [(side_ok, place(line, (row + step) % wide, core)) for step in range(1, wide)]

    def fan(k, src):
        rows = pl.ds(pl.multiple_of(k * chunk, chunk), chunk)
        for slot, (allowed, target) in enumerate(exits):
            pl.when(allowed)(lambda slot=slot, target=target: tree(slot, k, target)(src).start())
        for step in range(1, sticks):
            remote(src.at[rows], source.at[stick, rows], peer_send.at[step, k], peer_recv.at[step, k],
                   stick=(stick + step) % sticks).start()
        for step in range(1, cores):
            remote(src.at[rows], source.at[stick, rows], core_send.at[step, 0, k], core_recv.at[0, k],
                   band=place(line, row, (core + step) % cores)).start()

    def tree_arrival(k):
        rows = pl.ds(pl.multiple_of(k * chunk, chunk), chunk)
        return remote(source.at[stick, rows], source.at[stick, rows], tree_send.at[0, k], tree_recv.at[k],
                      band=place(line, (row + 1) % wide, core))

    def peer_copy(step, k):
        rows = pl.ds(pl.multiple_of(k * chunk, chunk), chunk)
        peer = (stick + step) % sticks
        return peer, remote(source.at[stick, rows], source.at[stick, rows], peer_send.at[step, k],
                            peer_recv.at[step, k], stick=peer)

    def relay(k):
        rows = pl.ds(pl.multiple_of(k * chunk, chunk), chunk)
        for step in range(1, sticks):
            peer_copy(step, k)[1].wait_recv()
            sender = (stick + sticks - step) % sticks
            for other in range(1, cores):
                remote(source.at[sender, rows], source.at[sender, rows], core_send.at[other, step, k],
                       core_recv.at[step, k], band=place(line, row, (core + other) % cores)).start()

    @pl.when(primary)
    def _():
        @pl.loop(0, CHUNKS)
        def _(k):
            @pl.when(is_root)
            def _():
                fan(k, piece)

            @pl.when(jnp.logical_not(is_root))
            def _():
                tree_arrival(k).wait_recv()
                fan(k, source.at[stick])

            for step in range(1, sticks):
                swap(step, k).start()
            pl.when(k > 0)(lambda: relay(k - 1))

        relay(CHUNKS - 1)

    @pl.when(jnp.logical_not(primary))
    def _():
        @pl.loop(0, CHUNKS)
        def _(k):
            for step in range(1, sticks):
                swap(step, k).start()

        @pl.loop(0, CHUNKS)
        def _(k):
            rows = pl.ds(pl.multiple_of(k * chunk, chunk), chunk)
            for step in range(sticks):
                sender = (stick + sticks - step) % sticks
                remote(source.at[sender, rows], source.at[sender, rows], core_send.at[0, step, k],
                       core_recv.at[step, k], band=place(line, row, (core + 1) % cores)).wait_recv()

    @pl.when(primary)
    def _():
        @pl.loop(0, CHUNKS)
        def _(k):
            for slot, (allowed, target) in enumerate(exits):
                pl.when(allowed)(lambda slot=slot, target=target: tree(slot, k, target)(piece).wait_send())
            for step in range(1, sticks):
                peer_copy(step, k)[1].wait_send()
            rows = pl.ds(pl.multiple_of(k * chunk, chunk), chunk)
            for other in range(1, cores):
                for step in range(sticks):
                    sender = (stick + sticks - step) % sticks
                    remote(source.at[sender, rows], source.at[sender, rows], core_send.at[other, step, k],
                           core_recv.at[step, k], band=place(line, row, (core + other) % cores)).wait_send()

    @pl.loop(0, CHUNKS)
    def _(k):
        for step in range(1, sticks):
            swap(step, k).wait()

    pl.when(is_root)(held.wait)
    keep.wait()


def spread(root, sticks, bands, piece, mine):
    capacity, depth = piece.shape
    shape = band_shape(bands)
    lines, wide, cores = shape
    dma = pltpu.SemaphoreType.DMA
    block = jax.ShapeDtypeStruct((sticks, capacity, depth), piece.dtype)
    anywhere = pl.BlockSpec(memory_space=pl.ANY)
    return pl.pallas_call(
        functools.partial(spread_kernel, root, sticks, shape, capacity // CHUNKS),
        out_shape=(block, block),
        in_specs=[anywhere, anywhere],
        out_specs=(anywhere, anywhere),
        scratch_shapes=[
            dma((2,)),
            dma((wide + 1, CHUNKS)),
            dma((CHUNKS,)),
            dma((sticks, CHUNKS)),
            dma((sticks, CHUNKS)),
            dma((cores, sticks, CHUNKS)),
            dma((sticks, CHUNKS)),
            dma((sticks, CHUNKS)),
            dma((sticks, CHUNKS)),
        ],
        compiler_params=pltpu.CompilerParams(collective_id=root, has_side_effects=True),
    )(piece, mine)


def spread_far(group, piece, mine):
    is_root = lax.axis_index("band") == group
    piece = lax.psum(jnp.where(is_root, piece, jnp.zeros_like(piece)), "band")
    source = lax.all_gather(piece, "stick", axis=0, tiled=False)
    owned = lax.all_to_all(mine, "stick", split_axis=0, concat_axis=0, tiled=True)
    return source, owned


def split(value):
    high = value.astype(jnp.bfloat16)
    low = (value - high.astype(jnp.float32)).astype(jnp.bfloat16)
    return high, low


def left(table, value):
    high, low = split(value)
    return jnp.dot(table, jnp.concatenate([high, low, high], axis=0), preferred_element_type=jnp.float32)


def along_z(value, table):
    high, low = split(value)
    both = jnp.dot(jnp.concatenate([high, low], axis=1), table, preferred_element_type=jnp.float32)
    return both[:, :NZ] + both[:, NZ:]


def exchange_kernel(sticks, capacity, perm, counts, owned, source, table_x, table_y, table_z, kernel, out,
                    pair_slot, source_slot, grid, source_grid, turned):
    rows = 128

    @pl.loop(0, sticks * capacity // rows)
    def _(i):
        at = pl.ds(pl.multiple_of(i * rows, rows), rows)
        value = source[at, :].astype(jnp.float32)
        source_slot[at, :] = value
        pair_slot[at, :] = owned[at, :].astype(jnp.float32) * value

    offset = 0
    for block in range(sticks):
        count = counts[block]

        def move(i, first, base):
            target = perm[first + i]
            grid[pl.ds(target, 1), :] = pair_slot[pl.ds(base + i, 1), :]
            source_grid[pl.ds(target, 1), :] = source_slot[pl.ds(base + i, 1), :]

        base = block * capacity

        @pl.loop(0, count // 16)
        def _(j):
            for u in range(16):
                move(j * 16 + u, offset, base)

        @pl.loop(count // 16 * 16, count)
        def _(i):
            move(i, offset, base)

        offset = offset + count

    def two(ref, first, length):
        a = ref[pl.ds(pl.multiple_of(first * length, length), length), :]
        b = ref[pl.ds(pl.multiple_of(first * length + length, length), length), :]
        return jnp.concatenate([a, b], axis=1)

    def turn(ref, value, first, many, stride):
        ref[pl.ds(first, many, stride=stride), :] = value[:, :NZ]
        ref[pl.ds(first + 1, many, stride=stride), :] = value[:, NZ:]

    def forward_y(i, _):
        turn(turned, left(table_y[...], two(grid, 2 * i, NY)), 2 * i, NY, NX)
        return 0

    lax.fori_loop(0, NX // 2, forward_y, 0, unroll=2)

    def middle(i, _):
        value = left(table_x[...], two(turned, 2 * i, NX))
        value = jnp.concatenate([value[:, :NZ], value[:, NZ:]], axis=0)
        value = along_z(value, table_z[...])
        value = value * kernel[pl.ds(pl.multiple_of(i * 2 * NX, 2 * NX), 2 * NX), :]
        value = along_z(value, table_z[...])
        value = jnp.concatenate([value[:NX], value[NX:]], axis=1)
        turn(grid, left(table_x[...], value), 2 * i, NX, NY)
        return 0

    lax.fori_loop(0, NY // 2, middle, 0, unroll=2)

    def inverse_y(i, _):
        value = left(table_y[...], two(grid, 2 * i, NY))
        at = pl.ds(pl.multiple_of(i * 2 * NY, 2 * NY), 2 * NY)
        value = jnp.concatenate([value[:, :NZ], value[:, NZ:]], axis=0)
        out[at, :] = (value * source_grid[at, :]).astype(jnp.bfloat16)
        return 0

    lax.fori_loop(0, NX // 2, inverse_y, 0, unroll=2)


def exchange(stick_perm, stick_counts, owned, source):
    sticks, capacity, depth = owned.shape
    table_x, low_x = halves(hartley_table(NX))
    table_y, low_y = halves(hartley_table(NY))
    table_z, low_z = halves(hartley_table(NZ))
    left_x = jnp.asarray(np.concatenate([table_x, table_x, low_x], axis=1))
    left_y = jnp.asarray(np.concatenate([table_y, table_y, low_y], axis=1))
    right_z = np.concatenate(
        [np.concatenate([table_z, low_z], axis=1), np.concatenate([table_z, np.zeros_like(low_z)], axis=1)], axis=0)
    right_z = jnp.asarray(right_z)
    kernel = screened(signed_freq(NX), signed_freq(NY), signed_freq(NZ)) * (-1.0 / (NX * NY * NZ))
    kernel = jnp.asarray(kernel.transpose(1, 0, 2).reshape(NX * NY, NZ), jnp.float32)
    smem = pl.BlockSpec(memory_space=pltpu.SMEM)
    vmem = pl.BlockSpec(memory_space=pltpu.VMEM)
    slots = sticks * capacity
    full = lambda n: pltpu.VMEM((n, NZ), jnp.float32)
    return pl.pallas_call(
        functools.partial(exchange_kernel, sticks, capacity),
        out_shape=jax.ShapeDtypeStruct((NX * NY, NZ), jnp.bfloat16),
        in_specs=[smem, smem] + [vmem] * 6,
        out_specs=vmem,
        scratch_shapes=[full(slots), full(slots), full(NX * NY), full(NX * NY), full(NX * NY)],
        compiler_params=pltpu.CompilerParams(vmem_limit_bytes=40 << 20),
    )(stick_perm, stick_counts, owned.reshape(slots, depth), source.reshape(slots, depth),
      left_x, left_y, right_z, kernel)


def local(orbital_sticks, stick_perm, stick_counts, source_ids):
    sticks = lax.axis_size("stick")
    bands = lax.axis_size("band")
    rows = orbital_sticks.shape[0]
    group = source_ids[0] // rows
    piece = lax.dynamic_index_in_dim(orbital_sticks, source_ids[0] % rows, 0, keepdims=False)
    if bands <= 16:
        branches = [functools.partial(spread, root, sticks, bands) for root in range(bands)]
        source, owned = lax.switch(group, branches, piece, orbital_sticks)
    else:
        source, owned = spread_far(group, piece, orbital_sticks)
    out = exchange(stick_perm, stick_counts, owned, source)
    return out.reshape(1, NX, NY, NZ)


def solution(mesh):
    placed = (P("band", "stick", None), P(), P(), P())
    return jax.shard_map(
        local,
        mesh=mesh,
        in_specs=placed,
        out_specs=P(("band", "stick"), None, None, None),
        check_vma=False,
    )
```

```python
import functools
import math

import jax
import jax.numpy as jnp
import numpy as np
from jax import lax
from jax.experimental import pallas as pl
from jax.experimental.pallas import tpu as pltpu
from jax.sharding import PartitionSpec as P

NX = 64
NY = 64
NZ = 128
CHUNKS = 8

screen_omega = 0.25


def signed_freq(length):
    steps = np.arange(length, dtype=np.int32)
    signed = np.where(steps <= length // 2, steps, steps - length)
    return signed.astype(np.float64) / length


def screened(freq_x, freq_y, freq_z):
    square = (2.0 * math.pi) ** 2 * (
        freq_x[:, None, None] ** 2 + freq_y[None, :, None] ** 2 + freq_z[None, None, :] ** 2
    )
    safe = np.where(square > 0, square, 1.0)
    inner = 4.0 * math.pi * (1.0 - np.exp(-square / (4.0 * screen_omega**2))) / safe
    return np.where(square > 0, inner, math.pi / screen_omega**2)


def hartley_table(length):
    steps = np.arange(length, dtype=np.int64)
    angle = (steps[:, None] * steps[None, :] % length) * (2.0 * math.pi / length)
    return np.cos(angle) + np.sin(angle)


def halves(table):
    high = table.astype(jnp.bfloat16)
    low = (table - high.astype(np.float64)).astype(jnp.bfloat16)
    return high, low


def band_shape(bands):
    return (bands // 4, 2, 2) if bands % 4 == 0 else (bands, 1, 1)


def spread_kernel(root, sticks, shape, chunk, piece, mine, source, owned, tree_send, tree_recv,
                  peer_send, peer_recv, core_send, core_recv, swap_send, swap_recv):
    lines, wide, cores = shape
    stick = lax.axis_index("stick")
    band = lax.axis_index("band")
    core = band % cores
    row = (band // cores) % wide
    line = band // (cores * wide)
    root_core = root % cores
    root_row = (root // cores) % wide
    root_line = root // (cores * wide)
    place = lambda l, r, c: (l * wide + r) * cores + c

    barrier = pltpu.get_barrier_semaphore()

    def greet(**where):
        pl.semaphore_signal(barrier, inc=1, device_id=where, device_id_type=pl.DeviceIdType.MESH)

    pl.when(line > 0)(lambda: greet(band=place(line - 1, row, core)))
    pl.when(line < lines - 1)(lambda: greet(band=place(line + 1, row, core)))
    for step in range(1, wide):
        greet(band=place(line, (row + step) % wide, core))
    for step in range(1, cores):
        greet(band=place(line, row, (core + step) % cores))
    for step in range(1, sticks):
        greet(stick=(stick + step) % sticks)
    near = jnp.where(line > 0, 1, 0) + jnp.where(line < lines - 1, 1, 0)
    pl.semaphore_wait(barrier, near + (wide - 1) + (cores - 1) + (sticks - 1))

    def remote(src, dst, send, recv, **where):
        return pltpu.make_async_remote_copy(
            src_ref=src, dst_ref=dst, send_sem=send, recv_sem=recv,
            device_id=where, device_id_type=pl.DeviceIdType.MESH)

    def swap(step, k):
        rows = pl.ds(pl.multiple_of(k * chunk, chunk), chunk)
        peer = (stick + step) % sticks
        return remote(mine.at[peer, rows], owned.at[stick, rows], swap_send.at[step, k], swap_recv.at[step, k],
                      stick=peer)

    primary = core == root_core
    is_root = band == root

    def tree(slot, k, target):
        rows = pl.ds(pl.multiple_of(k * chunk, chunk), chunk)
        return lambda src: remote(src.at[rows], source.at[stick, rows], tree_send.at[slot, k], tree_recv.at[k],
                                  band=target)

    up_ok = primary & (row == root_row) & (line >= root_line) & (line < lines - 1)
    down_ok = primary & (row == root_row) & (line <= root_line) & (line > 0)
    side_ok = primary & (row == root_row)
    exits = [(up_ok, place(line + 1, row, core)), (down_ok, place(line - 1, row, core))]
    exits += [(side_ok, place(line, (row + step) % wide, core)) for step in range(1, wide)]

    def fan(k, src):
        rows = pl.ds(pl.multiple_of(k * chunk, chunk), chunk)
        for slot, (allowed, target) in enumerate(exits):
            pl.when(allowed)(lambda slot=slot, target=target: tree(slot, k, target)(src).start())
        for step in range(1, sticks):
            remote(src.at[rows], source.at[stick, rows], peer_send.at[step, k], peer_recv.at[step, k],
                   stick=(stick + step) % sticks).start()
        for step in range(1, cores):
            remote(src.at[rows], source.at[stick, rows], core_send.at[step, 0, k], core_recv.at[0, k],
                   band=place(line, row, (core + step) % cores)).start()

    def tree_arrival(k):
        rows = pl.ds(pl.multiple_of(k * chunk, chunk), chunk)
        return remote(source.at[stick, rows], source.at[stick, rows], tree_send.at[0, k], tree_recv.at[k],
                      band=place(line, (row + 1) % wide, core))

    def peer_copy(step, k):
        rows = pl.ds(pl.multiple_of(k * chunk, chunk), chunk)
        peer = (stick + step) % sticks
        return peer, remote(source.at[stick, rows], source.at[stick, rows], peer_send.at[step, k],
                            peer_recv.at[step, k], stick=peer)

    def relay(k):
        rows = pl.ds(pl.multiple_of(k * chunk, chunk), chunk)
        for step in range(1, sticks):
            peer_copy(step, k)[1].wait_recv()
            sender = (stick + sticks - step) % sticks
            for other in range(1, cores):
                remote(source.at[sender, rows], source.at[sender, rows], core_send.at[other, step, k],
                       core_recv.at[step, k], band=place(line, row, (core + other) % cores)).start()

    @pl.when(primary)
    def _():
        @pl.loop(0, CHUNKS)
        def _(k):
            @pl.when(is_root)
            def _():
                fan(k, piece)

            @pl.when(jnp.logical_not(is_root))
            def _():
                tree_arrival(k).wait_recv()
                fan(k, source.at[stick])

            for step in range(1, sticks):
                swap(step, k).start()
            pl.when(k > 0)(lambda: relay(k - 1))

        relay(CHUNKS - 1)

    @pl.when(jnp.logical_not(primary))
    def _():
        @pl.loop(0, CHUNKS)
        def _(k):
            for step in range(1, sticks):
                swap(step, k).start()

        @pl.loop(0, CHUNKS)
        def _(k):
            rows = pl.ds(pl.multiple_of(k * chunk, chunk), chunk)
            for step in range(sticks):
                sender = (stick + sticks - step) % sticks
                remote(source.at[sender, rows], source.at[sender, rows], core_send.at[0, step, k],
                       core_recv.at[step, k], band=place(line, row, (core + 1) % cores)).wait_recv()

    @pl.when(primary)
    def _():
        @pl.loop(0, CHUNKS)
        def _(k):
            for slot, (allowed, target) in enumerate(exits):
                pl.when(allowed)(lambda slot=slot, target=target: tree(slot, k, target)(piece).wait_send())
            for step in range(1, sticks):
                peer_copy(step, k)[1].wait_send()
            rows = pl.ds(pl.multiple_of(k * chunk, chunk), chunk)
            for other in range(1, cores):
                for step in range(sticks):
                    sender = (stick + sticks - step) % sticks
                    remote(source.at[sender, rows], source.at[sender, rows], core_send.at[other, step, k],
                           core_recv.at[step, k], band=place(line, row, (core + other) % cores)).wait_send()

    @pl.loop(0, CHUNKS)
    def _(k):
        for step in range(1, sticks):
            swap(step, k).wait()


def spread(root, sticks, bands, piece, mine):
    capacity, depth = piece.shape
    shape = band_shape(bands)
    lines, wide, cores = shape
    dma = pltpu.SemaphoreType.DMA
    block = jax.ShapeDtypeStruct((sticks, capacity, depth), piece.dtype)
    anywhere = pl.BlockSpec(memory_space=pl.ANY)
    return pl.pallas_call(
        functools.partial(spread_kernel, root, sticks, shape, capacity // CHUNKS),
        out_shape=(block, block),
        in_specs=[anywhere, anywhere],
        out_specs=(anywhere, anywhere),
        scratch_shapes=[
            dma((wide + 1, CHUNKS)),
            dma((CHUNKS,)),
            dma((sticks, CHUNKS)),
            dma((sticks, CHUNKS)),
            dma((cores, sticks, CHUNKS)),
            dma((sticks, CHUNKS)),
            dma((sticks, CHUNKS)),
            dma((sticks, CHUNKS)),
        ],
        compiler_params=pltpu.CompilerParams(collective_id=root, has_side_effects=True),
    )(piece, mine)


def spread_far(group, piece, mine):
    is_root = lax.axis_index("band") == group
    piece = lax.psum(jnp.where(is_root, piece, jnp.zeros_like(piece)), "band")
    source = lax.all_gather(piece, "stick", axis=0, tiled=False)
    owned = lax.all_to_all(mine, "stick", split_axis=0, concat_axis=0, tiled=True)
    return source, owned


def split(value):
    high = value.astype(jnp.bfloat16)
    low = (value - high.astype(jnp.float32)).astype(jnp.bfloat16)
    return high, low


def left(table, value):
    high, low = split(value)
    return jnp.dot(table, jnp.concatenate([high, low, high], axis=0), preferred_element_type=jnp.float32)


def along_z(value, table):
    high, low = split(value)
    both = jnp.dot(jnp.concatenate([high, low], axis=1), table, preferred_element_type=jnp.float32)
    return both[:, :NZ] + both[:, NZ:]


def exchange_kernel(sticks, capacity, perm, counts, facts, owned_far, source_far, mine, table_x, table_y, table_z,
                    kernel, out, owned, source, sem, pair_slot, source_slot, grid, source_grid, turned):
    rows = 128
    stick, is_root, root_row = facts[0], facts[1], facts[2]

    def fetch(block):
        at = pl.ds(block * capacity, capacity)
        bring = lambda src, dst, which: pltpu.make_async_copy(src, dst.at[at], sem.at[which, block]).start()
        here = block == stick
        pl.when(here)(lambda: bring(mine.at[block], owned, 0))
        pl.when(jnp.logical_not(here))(lambda: bring(owned_far.at[block], owned, 0))
        from_mine = here & (is_root == 1)
        pl.when(from_mine)(lambda: bring(mine.at[root_row], source, 1))
        pl.when(jnp.logical_not(from_mine))(lambda: bring(source_far.at[block], source, 1))

    for block in range(sticks):
        fetch(block)

    offset = 0
    for block in range(sticks):
        count = counts[block]
        at_block = pl.ds(block * capacity, capacity)
        pltpu.make_async_copy(owned_far.at[block], owned.at[at_block], sem.at[0, block]).wait()
        pltpu.make_async_copy(source_far.at[block], source.at[at_block], sem.at[1, block]).wait()

        @pl.loop(0, capacity // rows)
        def _(i):
            at = pl.ds(pl.multiple_of(block * capacity + i * rows, rows), rows)
            value = source[at, :].astype(jnp.float32)
            source_slot[at, :] = value
            pair_slot[at, :] = owned[at, :].astype(jnp.float32) * value

        def move(i, first, base):
            target = perm[first + i]
            grid[pl.ds(target, 1), :] = pair_slot[pl.ds(base + i, 1), :]
            source_grid[pl.ds(target, 1), :] = source_slot[pl.ds(base + i, 1), :]

        base = block * capacity

        @pl.loop(0, count // 16)
        def _(j):
            for u in range(16):
                move(j * 16 + u, offset, base)

        @pl.loop(count // 16 * 16, count)
        def _(i):
            move(i, offset, base)

        offset = offset + count

    def two(ref, first, length):
        a = ref[pl.ds(pl.multiple_of(first * length, length), length), :]
        b = ref[pl.ds(pl.multiple_of(first * length + length, length), length), :]
        return jnp.concatenate([a, b], axis=1)

    def turn(ref, value, first, many, stride):
        ref[pl.ds(first, many, stride=stride), :] = value[:, :NZ]
        ref[pl.ds(first + 1, many, stride=stride), :] = value[:, NZ:]

    def forward_y(i, _):
        turn(turned, left(table_y[...], two(grid, 2 * i, NY)), 2 * i, NY, NX)
        return 0

    lax.fori_loop(0, NX // 2, forward_y, 0, unroll=16)

    def middle(i, _):
        value = left(table_x[...], two(turned, 2 * i, NX))
        value = jnp.concatenate([value[:, :NZ], value[:, NZ:]], axis=0)
        value = along_z(value, table_z[...])
        value = value * kernel[pl.ds(pl.multiple_of(i * 2 * NX, 2 * NX), 2 * NX), :]
        value = along_z(value, table_z[...])
        value = jnp.concatenate([value[:NX], value[NX:]], axis=1)
        turn(grid, left(table_x[...], value), 2 * i, NX, NY)
        return 0

    lax.fori_loop(0, NY // 2, middle, 0, unroll=8)

    def inverse_y(i, _):
        value = left(table_y[...], two(grid, 2 * i, NY))
        at = pl.ds(pl.multiple_of(i * 2 * NY, 2 * NY), 2 * NY)
        value = jnp.concatenate([value[:, :NZ], value[:, NZ:]], axis=0)
        out[at, :] = (value * source_grid[at, :]).astype(jnp.bfloat16)
        return 0

    lax.fori_loop(0, NX // 2, inverse_y, 0, unroll=16)


def exchange(stick_perm, stick_counts, facts, owned, source, mine):
    sticks, capacity, depth = owned.shape
    table_x, low_x = halves(hartley_table(NX))
    table_y, low_y = halves(hartley_table(NY))
    table_z, low_z = halves(hartley_table(NZ))
    left_x = jnp.asarray(np.concatenate([table_x, table_x, low_x], axis=1))
    left_y = jnp.asarray(np.concatenate([table_y, table_y, low_y], axis=1))
    right_z = np.concatenate(
        [np.concatenate([table_z, low_z], axis=1), np.concatenate([table_z, np.zeros_like(low_z)], axis=1)], axis=0)
    right_z = jnp.asarray(right_z)
    kernel = screened(signed_freq(NX), signed_freq(NY), signed_freq(NZ)) * (-1.0 / (NX * NY * NZ))
    kernel = jnp.asarray(kernel.transpose(1, 0, 2).reshape(NX * NY, NZ), jnp.float32)
    smem = pl.BlockSpec(memory_space=pltpu.SMEM)
    vmem = pl.BlockSpec(memory_space=pltpu.VMEM)
    anywhere = pl.BlockSpec(memory_space=pl.ANY)
    slots = sticks * capacity
    full = lambda n: pltpu.VMEM((n, NZ), jnp.float32)
    return pl.pallas_call(
        functools.partial(exchange_kernel, sticks, capacity),
        out_shape=jax.ShapeDtypeStruct((NX * NY, NZ), jnp.bfloat16),
        in_specs=[smem] * 3 + [anywhere] * 3 + [vmem] * 4,
        out_specs=vmem,
        scratch_shapes=[pltpu.VMEM((slots, NZ), jnp.bfloat16), pltpu.VMEM((slots, NZ), jnp.bfloat16),
                        pltpu.SemaphoreType.DMA((2, sticks)), full(slots), full(slots), full(NX * NY), full(NX * NY), full(NX * NY)],
        compiler_params=pltpu.CompilerParams(vmem_limit_bytes=40 << 20),
    )(stick_perm, stick_counts, facts, owned, source, mine,
      left_x, left_y, right_z, kernel)


def local(orbital_sticks, stick_perm, stick_counts, source_ids):
    sticks = lax.axis_size("stick")
    bands = lax.axis_size("band")
    rows = orbital_sticks.shape[0]
    group = source_ids[0] // rows
    piece = lax.dynamic_index_in_dim(orbital_sticks, source_ids[0] % rows, 0, keepdims=False)
    if bands <= 16:
        branches = [functools.partial(spread, root, sticks, bands) for root in range(bands)]
        source, owned = lax.switch(group, branches, piece, orbital_sticks)
    else:
        source, owned = spread_far(group, piece, orbital_sticks)
    row = source_ids[0] % rows
    is_root = (lax.axis_index("band") == group).astype(jnp.int32)
    facts = jnp.stack([lax.axis_index("stick"), is_root, row]).astype(jnp.int32)
    out = exchange(stick_perm, stick_counts, facts, owned, source, orbital_sticks)
    return out.reshape(1, NX, NY, NZ)


def solution(mesh):
    placed = (P("band", "stick", None), P(), P(), P())
    return jax.shard_map(
        local,
        mesh=mesh,
        in_specs=placed,
        out_specs=P(("band", "stick"), None, None, None),
        check_vma=False,
    )
```

```python
import functools
import math

import jax
import jax.numpy as jnp
import numpy as np
from jax import lax
from jax.experimental import pallas as pl
from jax.experimental.pallas import tpu as pltpu
from jax.sharding import PartitionSpec as P

NX = 64
NY = 64
NZ = 128
CHUNKS = 8
LAG = 3

screen_omega = 0.25


def signed_freq(length):
    steps = np.arange(length, dtype=np.int32)
    signed = np.where(steps <= length // 2, steps, steps - length)
    return signed.astype(np.float64) / length


def screened(freq_x, freq_y, freq_z):
    square = (2.0 * math.pi) ** 2 * (
        freq_x[:, None, None] ** 2 + freq_y[None, :, None] ** 2 + freq_z[None, None, :] ** 2
    )
    safe = np.where(square > 0, square, 1.0)
    inner = 4.0 * math.pi * (1.0 - np.exp(-square / (4.0 * screen_omega**2))) / safe
    return np.where(square > 0, inner, math.pi / screen_omega**2)


def hartley_table(length):
    steps = np.arange(length, dtype=np.int64)
    angle = (steps[:, None] * steps[None, :] % length) * (2.0 * math.pi / length)
    return np.cos(angle) + np.sin(angle)


def halves(table):
    high = table.astype(jnp.bfloat16)
    low = (table - high.astype(np.float64)).astype(jnp.bfloat16)
    return high, low


def band_shape(bands):
    return (bands // 4, 2, 2) if bands % 4 == 0 else (bands, 1, 1)


def spread_kernel(root, sticks, shape, chunk, piece, mine, source, owned, tree_send, tree_recv,
                  peer_send, peer_recv, core_send, core_recv, swap_send, swap_recv):
    lines, wide, cores = shape
    stick = lax.axis_index("stick")
    band = lax.axis_index("band")
    core = band % cores
    row = (band // cores) % wide
    line = band // (cores * wide)
    root_core = root % cores
    root_row = (root // cores) % wide
    root_line = root // (cores * wide)
    place = lambda l, r, c: (l * wide + r) * cores + c

    barrier = pltpu.get_barrier_semaphore()

    def greet(**where):
        pl.semaphore_signal(barrier, inc=1, device_id=where, device_id_type=pl.DeviceIdType.MESH)

    pl.when(line > 0)(lambda: greet(band=place(line - 1, row, core)))
    pl.when(line < lines - 1)(lambda: greet(band=place(line + 1, row, core)))
    for step in range(1, wide):
        greet(band=place(line, (row + step) % wide, core))
    for step in range(1, cores):
        greet(band=place(line, row, (core + step) % cores))
    for step in range(1, sticks):
        greet(stick=(stick + step) % sticks)
    near = jnp.where(line > 0, 1, 0) + jnp.where(line < lines - 1, 1, 0)
    pl.semaphore_wait(barrier, near + (wide - 1) + (cores - 1) + (sticks - 1))

    def remote(src, dst, send, recv, **where):
        return pltpu.make_async_remote_copy(
            src_ref=src, dst_ref=dst, send_sem=send, recv_sem=recv,
            device_id=where, device_id_type=pl.DeviceIdType.MESH)

    def swap(step, k):
        rows = pl.ds(pl.multiple_of(k * chunk, chunk), chunk)
        peer = (stick + step) % sticks
        return remote(mine.at[peer, rows], owned.at[stick, rows], swap_send.at[step, k], swap_recv.at[step, k],
                      stick=peer)

    primary = core == root_core
    is_root = band == root

    def tree(slot, k, target):
        rows = pl.ds(pl.multiple_of(k * chunk, chunk), chunk)
        return lambda src: remote(src.at[rows], source.at[stick, rows], tree_send.at[slot, k], tree_recv.at[k],
                                  band=target)

    up_ok = primary & (row == root_row) & (line >= root_line) & (line < lines - 1)
    down_ok = primary & (row == root_row) & (line <= root_line) & (line > 0)
    side_ok = primary & (row == root_row)
    exits = [(up_ok, place(line + 1, row, core)), (down_ok, place(line - 1, row, core))]
    exits += [(side_ok, place(line, (row + step) % wide, core)) for step in range(1, wide)]

    def fan(k, src):
        rows = pl.ds(pl.multiple_of(k * chunk, chunk), chunk)
        for slot, (allowed, target) in enumerate(exits):
            pl.when(allowed)(lambda slot=slot, target=target: tree(slot, k, target)(src).start())
        for step in range(1, sticks):
            remote(src.at[rows], source.at[stick, rows], peer_send.at[step, k], peer_recv.at[step, k],
                   stick=(stick + step) % sticks).start()
        for step in range(1, cores):
            remote(src.at[rows], source.at[stick, rows], core_send.at[step, 0, k], core_recv.at[0, k],
                   band=place(line, row, (core + step) % cores)).start()

    def tree_arrival(k):
        rows = pl.ds(pl.multiple_of(k * chunk, chunk), chunk)
        return remote(source.at[stick, rows], source.at[stick, rows], tree_send.at[0, k], tree_recv.at[k],
                      band=place(line, (row + 1) % wide, core))

    def peer_copy(step, k):
        rows = pl.ds(pl.multiple_of(k * chunk, chunk), chunk)
        peer = (stick + step) % sticks
        return peer, remote(source.at[stick, rows], source.at[stick, rows], peer_send.at[step, k],
                            peer_recv.at[step, k], stick=peer)

    def relay(k):
        rows = pl.ds(pl.multiple_of(k * chunk, chunk), chunk)
        for step in range(1, sticks):
            peer_copy(step, k)[1].wait_recv()
            sender = (stick + sticks - step) % sticks
            for other in range(1, cores):
                remote(source.at[sender, rows], source.at[sender, rows], core_send.at[other, step, k],
                       core_recv.at[step, k], band=place(line, row, (core + other) % cores)).start()

    @pl.when(primary)
    def _():
        @pl.loop(0, CHUNKS)
        def _(k):
            @pl.when(is_root)
            def _():
                fan(k, piece)

            @pl.when(jnp.logical_not(is_root))
            def _():
                tree_arrival(k).wait_recv()
                fan(k, source.at[stick])

            for step in range(1, sticks):
                swap(step, k).start()
            pl.when(k >= LAG)(lambda: relay(k - LAG))

        @pl.loop(CHUNKS - LAG, CHUNKS)
        def _(k):
            relay(k)

    @pl.when(jnp.logical_not(primary))
    def _():
        @pl.loop(0, CHUNKS)
        def _(k):
            for step in range(1, sticks):
                swap(step, k).start()

        @pl.loop(0, CHUNKS)
        def _(k):
            rows = pl.ds(pl.multiple_of(k * chunk, chunk), chunk)
            for step in range(sticks):
                sender = (stick + sticks - step) % sticks
                remote(source.at[sender, rows], source.at[sender, rows], core_send.at[0, step, k],
                       core_recv.at[step, k], band=place(line, row, (core + 1) % cores)).wait_recv()

    @pl.when(primary)
    def _():
        @pl.loop(0, CHUNKS)
        def _(k):
            for slot, (allowed, target) in enumerate(exits):
                pl.when(allowed)(lambda slot=slot, target=target: tree(slot, k, target)(piece).wait_send())
            for step in range(1, sticks):
                peer_copy(step, k)[1].wait_send()
            rows = pl.ds(pl.multiple_of(k * chunk, chunk), chunk)
            for other in range(1, cores):
                for step in range(sticks):
                    sender = (stick + sticks - step) % sticks
                    remote(source.at[sender, rows], source.at[sender, rows], core_send.at[other, step, k],
                           core_recv.at[step, k], band=place(line, row, (core + other) % cores)).wait_send()

    @pl.loop(0, CHUNKS)
    def _(k):
        for step in range(1, sticks):
            swap(step, k).wait()


def spread(root, sticks, bands, piece, mine):
    capacity, depth = piece.shape
    shape = band_shape(bands)
    lines, wide, cores = shape
    dma = pltpu.SemaphoreType.DMA
    block = jax.ShapeDtypeStruct((sticks, capacity, depth), piece.dtype)
    anywhere = pl.BlockSpec(memory_space=pl.ANY)
    return pl.pallas_call(
        functools.partial(spread_kernel, root, sticks, shape, capacity // CHUNKS),
        out_shape=(block, block),
        in_specs=[anywhere, anywhere],
        out_specs=(anywhere, anywhere),
        scratch_shapes=[
            dma((wide + 1, CHUNKS)),
            dma((CHUNKS,)),
            dma((sticks, CHUNKS)),
            dma((sticks, CHUNKS)),
            dma((cores, sticks, CHUNKS)),
            dma((sticks, CHUNKS)),
            dma((sticks, CHUNKS)),
            dma((sticks, CHUNKS)),
        ],
        compiler_params=pltpu.CompilerParams(collective_id=root, has_side_effects=True),
    )(piece, mine)


def spread_far(group, piece, mine):
    is_root = lax.axis_index("band") == group
    piece = lax.psum(jnp.where(is_root, piece, jnp.zeros_like(piece)), "band")
    source = lax.all_gather(piece, "stick", axis=0, tiled=False)
    owned = lax.all_to_all(mine, "stick", split_axis=0, concat_axis=0, tiled=True)
    return source, owned


def split(value):
    high = value.astype(jnp.bfloat16)
    low = (value - high.astype(jnp.float32)).astype(jnp.bfloat16)
    return high, low


def left(table, value):
    high, low = split(value)
    return jnp.dot(table, jnp.concatenate([high, low, high], axis=0), preferred_element_type=jnp.float32)


def along_z(value, table):
    high, low = split(value)
    both = jnp.dot(jnp.concatenate([high, low], axis=1), table, preferred_element_type=jnp.float32)
    return both[:, :NZ] + both[:, NZ:]


def exchange_kernel(sticks, capacity, perm, counts, facts, owned_far, source_far, mine, table_x, table_y, table_z,
                    kernel, out, owned, source, sem, pair_slot, source_slot, grid, source_grid, turned):
    rows = 128
    stick, is_root, root_row = facts[0], facts[1], facts[2]

    def fetch(block):
        at = pl.ds(block * capacity, capacity)
        bring = lambda src, dst, which: pltpu.make_async_copy(src, dst.at[at], sem.at[which, block]).start()
        here = block == stick
        pl.when(here)(lambda: bring(mine.at[block], owned, 0))
        pl.when(jnp.logical_not(here))(lambda: bring(owned_far.at[block], owned, 0))
        from_mine = here & (is_root == 1)
        pl.when(from_mine)(lambda: bring(mine.at[root_row], source, 1))
        pl.when(jnp.logical_not(from_mine))(lambda: bring(source_far.at[block], source, 1))

    for block in range(sticks):
        fetch(block)

    offset = 0
    for block in range(sticks):
        count = counts[block]
        at_block = pl.ds(block * capacity, capacity)
        pltpu.make_async_copy(owned_far.at[block], owned.at[at_block], sem.at[0, block]).wait()
        pltpu.make_async_copy(source_far.at[block], source.at[at_block], sem.at[1, block]).wait()

        @pl.loop(0, capacity // rows)
        def _(i):
            at = pl.ds(pl.multiple_of(block * capacity + i * rows, rows), rows)
            value = source[at, :].astype(jnp.float32)
            source_slot[at, :] = value
            pair_slot[at, :] = owned[at, :].astype(jnp.float32) * value

        def move(i, first, base):
            target = perm[first + i]
            grid[pl.ds(target, 1), :] = pair_slot[pl.ds(base + i, 1), :]
            source_grid[pl.ds(target, 1), :] = source_slot[pl.ds(base + i, 1), :]

        base = block * capacity

        @pl.loop(0, count // 16)
        def _(j):
            for u in range(16):
                move(j * 16 + u, offset, base)

        @pl.loop(count // 16 * 16, count)
        def _(i):
            move(i, offset, base)

        offset = offset + count

    def two(ref, first, length):
        a = ref[pl.ds(pl.multiple_of(first * length, length), length), :]
        b = ref[pl.ds(pl.multiple_of(first * length + length, length), length), :]
        return jnp.concatenate([a, b], axis=1)

    def turn(ref, value, first, many, stride):
        ref[pl.ds(first, many, stride=stride), :] = value[:, :NZ]
        ref[pl.ds(first + 1, many, stride=stride), :] = value[:, NZ:]

    def forward_y(i, _):
        turn(turned, left(table_y[...], two(grid, 2 * i, NY)), 2 * i, NY, NX)
        return 0

    lax.fori_loop(0, NX // 2, forward_y, 0, unroll=16)

    def middle(i, _):
        value = left(table_x[...], two(turned, 2 * i, NX))
        value = jnp.concatenate([value[:, :NZ], value[:, NZ:]], axis=0)
        value = along_z(value, table_z[...])
        value = value * kernel[pl.ds(pl.multiple_of(i * 2 * NX, 2 * NX), 2 * NX), :]
        value = along_z(value, table_z[...])
        value = jnp.concatenate([value[:NX], value[NX:]], axis=1)
        turn(grid, left(table_x[...], value), 2 * i, NX, NY)
        return 0

    lax.fori_loop(0, NY // 2, middle, 0, unroll=8)

    def inverse_y(i, _):
        value = left(table_y[...], two(grid, 2 * i, NY))
        at = pl.ds(pl.multiple_of(i * 2 * NY, 2 * NY), 2 * NY)
        value = jnp.concatenate([value[:, :NZ], value[:, NZ:]], axis=0)
        out[at, :] = (value * source_grid[at, :]).astype(jnp.bfloat16)
        return 0

    lax.fori_loop(0, NX // 2, inverse_y, 0, unroll=16)


def exchange(stick_perm, stick_counts, facts, owned, source, mine):
    sticks, capacity, depth = owned.shape
    table_x, low_x = halves(hartley_table(NX))
    table_y, low_y = halves(hartley_table(NY))
    table_z, low_z = halves(hartley_table(NZ))
    left_x = jnp.asarray(np.concatenate([table_x, table_x, low_x], axis=1))
    left_y = jnp.asarray(np.concatenate([table_y, table_y, low_y], axis=1))
    right_z = np.concatenate(
        [np.concatenate([table_z, low_z], axis=1), np.concatenate([table_z, np.zeros_like(low_z)], axis=1)], axis=0)
    right_z = jnp.asarray(right_z)
    kernel = screened(signed_freq(NX), signed_freq(NY), signed_freq(NZ)) * (-1.0 / (NX * NY * NZ))
    kernel = jnp.asarray(kernel.transpose(1, 0, 2).reshape(NX * NY, NZ), jnp.float32)
    smem = pl.BlockSpec(memory_space=pltpu.SMEM)
    vmem = pl.BlockSpec(memory_space=pltpu.VMEM)
    anywhere = pl.BlockSpec(memory_space=pl.ANY)
    slots = sticks * capacity
    full = lambda n: pltpu.VMEM((n, NZ), jnp.float32)
    return pl.pallas_call(
        functools.partial(exchange_kernel, sticks, capacity),
        out_shape=jax.ShapeDtypeStruct((NX * NY, NZ), jnp.bfloat16),
        in_specs=[smem] * 3 + [anywhere] * 3 + [vmem] * 4,
        out_specs=vmem,
        scratch_shapes=[pltpu.VMEM((slots, NZ), jnp.bfloat16), pltpu.VMEM((slots, NZ), jnp.bfloat16),
                        pltpu.SemaphoreType.DMA((2, sticks)), full(slots), full(slots), full(NX * NY), full(NX * NY), full(NX * NY)],
        compiler_params=pltpu.CompilerParams(vmem_limit_bytes=40 << 20),
    )(stick_perm, stick_counts, facts, owned, source, mine,
      left_x, left_y, right_z, kernel)


def local(orbital_sticks, stick_perm, stick_counts, source_ids):
    sticks = lax.axis_size("stick")
    bands = lax.axis_size("band")
    rows = orbital_sticks.shape[0]
    group = source_ids[0] // rows
    piece = lax.dynamic_index_in_dim(orbital_sticks, source_ids[0] % rows, 0, keepdims=False)
    if bands <= 16:
        branches = [functools.partial(spread, root, sticks, bands) for root in range(bands)]
        source, owned = lax.switch(group, branches, piece, orbital_sticks)
    else:
        source, owned = spread_far(group, piece, orbital_sticks)
    row = source_ids[0] % rows
    is_root = (lax.axis_index("band") == group).astype(jnp.int32)
    facts = jnp.stack([lax.axis_index("stick"), is_root, row]).astype(jnp.int32)
    out = exchange(stick_perm, stick_counts, facts, owned, source, orbital_sticks)
    return out.reshape(1, NX, NY, NZ)


def solution(mesh):
    placed = (P("band", "stick", None), P(), P(), P())
    return jax.shard_map(
        local,
        mesh=mesh,
        in_specs=placed,
        out_specs=P(("band", "stick"), None, None, None),
        check_vma=False,
    )
```
